256 devices in a mesh: row: 16 (over z, core), col: 16 (over x, y).
Axes of the slice: x: 4, y: 4, z: 8, core: 2. Of those that a mesh axis runs over, the one named last changes fastest.
Arguments:
- eigvec: float32 [32768, 8192], P('row', 'col'), may hold values from -6 to 6
- slots: float32 [16, 32768, 256], P('col', 'row'), may hold values from -0.03125 to 0.03125
- roots: int32 [3], replicated, may hold values from 0 to 15, as said below
- tfac: float32 [3, 256, 256], replicated, as said below
Outputs:
- transformed: float32 [32768, 8192], P('row', 'col')
The draws below stay inside these ranges and needn't reach their ends.
Inputs may be any that keep to these rules, and one draw needn't show every extreme that they name: The panels lie in consecutive grid columns, roots[k] = (roots[0] + k) mod 16; roots[0] is one of the last two grid columns, so the panels always wrap past the last grid column. tfac[k] is upper triangular with a diagonal between 1 and 2.
All inputs are finite; a program needn't handle non-finite values.
Results may differ from the reference program's by a relative error of at most 0.00013.
Values sent between devices are 32-bit elements; how exact they have to be, the bound alone decides.
A program may use at most 64 MiB of HBM per device.

```python
import jax
import jax.numpy as jnp
from jax import lax

NB = 256
NE = 8192
PANELS = 3
ROWS = 32768
GRID_COLS = 16


def draw_roots(key, part):
    start = jax.random.randint(key, (), GRID_COLS - 2, GRID_COLS)
    return ((start + jnp.arange(PANELS)) % GRID_COLS).astype(jnp.int32)


def draw_tfac(key, part):
    key_diag, key_off = jax.random.split(jax.random.fold_in(key, 17))
    diag = jax.random.uniform(key_diag, (PANELS, NB), jnp.float32, 1.0, 2.0)
    off = jax.random.normal(key_off, (PANELS, NB, NB), jnp.float32) * (0.6 / jnp.sqrt(NB * 1.0))
    upper = jnp.triu(off, 1)
    return upper + diag[:, :, None] * jnp.eye(NB, dtype=jnp.float32)[None]


def steps_of(own_key, shape, cuts, least, top_value):
    gain, own = 1.0, jax.random.fold_in(own_key, 6)
    for dim, blocks in cuts:
        steps = jnp.exp(jax.random.uniform(jax.random.fold_in(own, dim), (blocks,), jnp.float32, least / len(cuts), top_value / len(cuts)))
        gain = gain * jnp.repeat(steps, shape[dim] // blocks).reshape([-1 if axis == dim else 1 for axis in range(len(shape))])
    return gain


def bell_draw(key, shape, deviation, bound, shards=(), held_as=jnp.bfloat16):
    drawn = jax.random.normal(key, shape, jnp.float32) * deviation
    if len(shards) > 0:
        drawn = steps_of(key, shape, shards, -0.22, 0.18) * drawn
    return jnp.clip(drawn, min=-bound, max=bound).astype(held_as)


def setup_inputs(seed: int = 0) -> dict:
    seeds = jax.random.split(jax.random.key(seed), 5)
    return {
        "eigvec": bell_draw(seeds[0], (ROWS, NE), 1.0, 6.0, ((0, 16), (1, 16)), jnp.float32),
        "slots": bell_draw(seeds[1], (GRID_COLS, ROWS, NB), ROWS ** -0.5, 0.03125, ((0, 16), (1, 16)), jnp.float32),
        "roots": draw_roots(jax.random.fold_in(seeds[4], 71), 0),
        "tfac": draw_tfac(jax.random.fold_in(seeds[4], 71), 0),
    }


def reference(eigvec, slots, roots, tfac):
    current = eigvec
    for index in range(PANELS):
        panel = slots[roots[index]]
        inner = jnp.dot(panel.T, current, precision=lax.Precision.HIGHEST, preferred_element_type=jnp.float32)
        scaled = jnp.dot(tfac[index], inner, precision=lax.Precision.HIGHEST, preferred_element_type=jnp.float32)
        current = current - jnp.dot(panel, scaled, precision=lax.Precision.HIGHEST, preferred_element_type=jnp.float32)
    return current
```

```python
import functools

import jax
import jax.numpy as jnp
from jax import lax
from jax.experimental import pallas as pl
from jax.experimental.pallas import tpu as pltpu
from jax.sharding import PartitionSpec as P

PANELS = 3
NB = 256
SIDE = 4
TREES = 4
HOPS = 5
CHUNK = 32
SKEW = 4
MESH = pl.DeviceIdType.MESH

FEED = {
    (0, 1): 0, (0, 2): 0, (0, 3): 0, (1, 0): 2, (1, 1): 2, (1, 2): 2, (1, 3): 2, (2, 0): 2,
    (2, 1): 1, (2, 2): 1, (2, 3): 2, (3, 0): 2, (3, 1): 1, (3, 2): 3, (3, 3): 3,
}
STEP = ((1, 0), (0, 1), (-1, 0), (0, -1))


def turn(node, times):
    for _ in range(times):
        node = (-node[1] % SIDE, node[0])
    return node


def build_tables():
    depth = {(0, 0): 0}

    def find(node):
        if node not in depth:
            dx, dy = STEP[FEED[node]]
            depth[node] = 1 + find(((node[0] - dx) % SIDE, (node[1] - dy) % SIDE))
        return depth[node]

    child = [[0] * 4 for _ in range(TREES)]
    deeper = [[0] * HOPS for _ in range(TREES)]
    for node in FEED:
        find(node)
        dx, dy = STEP[FEED[node]]
        parent = ((node[0] - dx) % SIDE, (node[1] - dy) % SIDE)
        for t in range(TREES):
            px, py = turn(parent, t)
            child[t][(FEED[node] + t) % 4] |= 1 << (px * SIDE + py)
            nx, ny = turn(node, t)
            for level in range(depth[node]):
                deeper[t][level] |= 1 << (nx * SIDE + ny)
    return child, deeper


CHILD, DEEPER = build_tables()


def bit(mask, place):
    return lax.rem(lax.shift_right_logical(jnp.int32(mask), place), 2)


def spread_kernel(roots, slot_ref, panel_ref, send_sem, recv_sem, load_sem):
    col = lax.axis_index("col")
    x, y = col // SIDE, lax.rem(col, SIDE)
    near = [
        lax.rem(x + 1, SIDE) * SIDE + y,
        x * SIDE + lax.rem(y + 1, SIDE),
        lax.rem(x + 3, SIDE) * SIDE + y,
        x * SIDE + lax.rem(y + 3, SIDE),
    ]
    rows = panel_ref.shape[1]
    count = rows // (TREES * CHUNK)

    barrier = pltpu.get_barrier_semaphore()
    for d in range(4):
        pl.semaphore_signal(barrier, inc=1, device_id={"col": near[d]}, device_id_type=MESH)

    place = []
    for p in range(PANELS):
        rx, ry = roots[p] // SIDE, roots[p] % SIDE
        place.append(lax.rem(x - rx + SIDE, SIDE) * SIDE + lax.rem(y - ry + SIDE, SIDE))
        load = pltpu.make_async_copy(slot_ref.at[0], panel_ref.at[p], load_sem)

        @pl.when(place[p] == 0)
        def _():
            load.start()
            load.wait()

    pl.semaphore_wait(barrier, 4)
    level = [[sum(bit(m, place[p]) for m in DEEPER[t]) for t in range(TREES)] for p in range(PANELS)]

    def piece(p, c, t, d):
        block = panel_ref.at[p, pl.ds(pl.multiple_of((c * TREES + t) * CHUNK, CHUNK), CHUNK)]
        return pltpu.make_async_remote_copy(
            src_ref=block,
            dst_ref=block,
            send_sem=send_sem.at[p, t, d],
            recv_sem=recv_sem.at[p, c, t],
            device_id={"col": near[d]},
            device_id_type=MESH,
        )

    def step(s, carry):
        for p in range(PANELS):
            for t in range(TREES):
                c = s - p * count - SKEW * level[p][t]

                @pl.when(jnp.logical_and(c >= 0, c < count))
                def _():
                    @pl.when(place[p] != 0)
                    def _():
                        piece(p, c, t, 0).wait_recv()

                    for d in range(4):
                        @pl.when(bit(CHILD[t][d], place[p]) == 1)
                        def _():
                            piece(p, c, t, d).start()
        return carry

    lax.fori_loop(0, PANELS * count + SKEW * HOPS, step, 0)

    for p in range(PANELS):
        for t in range(TREES):
            for d in range(4):
                @pl.when(bit(CHILD[t][d], place[p]) == 1)
                def _():
                    whole = panel_ref.at[p, pl.ds(0, rows // TREES)]
                    pltpu.make_async_remote_copy(
                        src_ref=whole,
                        dst_ref=whole,
                        send_sem=send_sem.at[p, t, d],
                        recv_sem=recv_sem.at[p, 0, t],
                        device_id={"col": near[d]},
                        device_id_type=MESH,
                    ).wait_send()


def spread(roots, key, slot):
    rows = slot.shape[1]
    count = rows // (TREES * CHUNK)
    return pl.pallas_call(
        functools.partial(spread_kernel, roots),
        out_shape=jax.ShapeDtypeStruct((PANELS, rows, NB), jnp.float32),
        in_specs=[pl.BlockSpec(memory_space=pl.ANY)],
        out_specs=pl.BlockSpec(memory_space=pltpu.VMEM),
        scratch_shapes=[
            pltpu.SemaphoreType.DMA((PANELS, TREES, 4)),
            pltpu.SemaphoreType.DMA((PANELS, count, TREES)),
            pltpu.SemaphoreType.DMA,
        ],
        compiler_params=pltpu.CompilerParams(collective_id=key, has_side_effects=True),
        name="spread_%d" % key,
    )(slot)


def product(left, right, dims):
    return lax.dot_general(
        left, right, (dims, ((), ())), precision=lax.Precision.HIGH, preferred_element_type=jnp.float32
    )


def shards(eigvec, slots, roots, tfac):
    panels = lax.cond(
        roots[0] == 14,
        functools.partial(spread, (14, 15, 0), 0),
        functools.partial(spread, (15, 0, 1), 1),
        slots,
    )
    first, second, third = panels[0], panels[1], panels[2]
    down = ((0,), (0,))
    inner = [product(v, eigvec, down) for v in (first, second, third)]
    cross = [product(second, first, down), product(third, first, down), product(third, second, down)]
    inner, cross = lax.psum((inner, cross), "row")
    flat = ((1,), (0,))
    y1 = product(tfac[0], inner[0], flat)
    y2 = product(tfac[1], inner[1] - product(cross[0], y1, flat), flat)
    y3 = product(tfac[2], inner[2] - product(cross[1], y1, flat) - product(cross[2], y2, flat), flat)
    return eigvec - (product(first, y1, flat) + product(second, y2, flat) + product(third, y3, flat))


def solution(mesh):
    in_specs = (P("row", "col"), P("col", "row", None), P(), P())
    out_specs = P("row", "col")
    return jax.shard_map(shards, mesh=mesh, in_specs=in_specs, out_specs=out_specs, check_vma=False)
```

```python
import functools

import jax
import jax.numpy as jnp
from jax import lax
from jax.experimental import pallas as pl
from jax.experimental.pallas import tpu as pltpu
from jax.sharding import PartitionSpec as P

PANELS = 3
NB = 256
SIDE = 4
TREES = 4
HOPS = 5
CHUNK = 32
SKEW = 4
GRID = SIDE * SIDE
DEPTH = 8
HALF = NB // 2
PREP = 16
GAPS = (3, 14, 26, 29)
MESH = pl.DeviceIdType.MESH

FEED = {
    (0, 1): 0, (0, 2): 0, (0, 3): 0, (1, 0): 2, (1, 1): 2, (1, 2): 2, (1, 3): 2, (2, 0): 2,
    (2, 1): 1, (2, 2): 1, (2, 3): 2, (3, 0): 2, (3, 1): 1, (3, 2): 3, (3, 3): 3,
}
STEP = ((1, 0), (0, 1), (-1, 0), (0, -1))


def turn(node, times):
    for _ in range(times):
        node = (-node[1] % SIDE, node[0])
    return node


def build_tables():
    depth = {(0, 0): 0}

    def find(node):
        if node not in depth:
            dx, dy = STEP[FEED[node]]
            depth[node] = 1 + find(((node[0] - dx) % SIDE, (node[1] - dy) % SIDE))
        return depth[node]

    child = [[0] * 4 for _ in range(TREES)]
    deeper = [[0] * HOPS for _ in range(TREES)]
    for node in FEED:
        find(node)
        dx, dy = STEP[FEED[node]]
        parent = ((node[0] - dx) % SIDE, (node[1] - dy) % SIDE)
        for t in range(TREES):
            px, py = turn(parent, t)
            child[t][(FEED[node] + t) % 4] |= 1 << (px * SIDE + py)
            nx, ny = turn(node, t)
            for level in range(depth[node]):
                deeper[t][level] |= 1 << (nx * SIDE + ny)
    return child, deeper


CHILD, DEEPER = build_tables()


def bit(mask, place):
    return lax.rem(lax.shift_right_logical(jnp.int32(mask), place), 2)


def split(value):
    high = value.astype(jnp.bfloat16)
    return high, (value - high.astype(jnp.float32)).astype(jnp.bfloat16)


def dot(left, right, turned=False):
    dims = ((1,), (1,)) if turned else ((1,), (0,))
    return lax.dot_general(left, right, (dims, ((), ())), preferred_element_type=jnp.float32)


def dot3(left, right, turned=False):
    return dot(left[0], right[0], turned) + (dot(left[0], right[1], turned) + dot(left[1], right[0], turned))


def kernel(
    roots, slot_ref, x_ref, t_ref, out_ref,
    panel, state, xh, xl, vh, vl, acc, fromcore, chip, fromz, crossz, total, cross, yth, ytl, yh, yl,
    tree_send, tree_recv, load_sem, core_send, core_recv, z_send, z_recv, cz_send, cz_recv,
    all_send, all_recv, relay_send, relay_recv, plane_send, plane_recv, pass_send, pass_recv, out_sem,
):
    row, col = lax.axis_index("row"), lax.axis_index("col")
    x, y = col // SIDE, lax.rem(col, SIDE)
    z, core = row // 2, lax.rem(row, 2)
    near = [
        lax.rem(x + 1, SIDE) * SIDE + y,
        x * SIDE + lax.rem(y + 1, SIDE),
        lax.rem(x + 3, SIDE) * SIDE + y,
        x * SIDE + lax.rem(y + 3, SIDE),
    ]
    mate = {"row": z * 2 + 1 - core}
    rows, width = state.shape
    block = TREES * CHUNK
    count = rows // block

    def zplus(k):
        return lax.rem(z + k, DEPTH)

    load_x = pltpu.make_async_copy(x_ref, state, load_sem.at[0])
    load_x.start()

    barrier = pltpu.get_barrier_semaphore()
    for k in range(1, GRID):
        pl.semaphore_signal(barrier, inc=1, device_id={"col": lax.rem(col + k, GRID)}, device_id_type=MESH)
    for k in range(1, DEPTH):
        pl.semaphore_signal(barrier, inc=1, device_id={"row": zplus(k) * 2 + core}, device_id_type=MESH)
    pl.semaphore_signal(barrier, inc=1, device_id=mate, device_id_type=MESH)

    place = []
    for p in range(PANELS):
        rx, ry = roots[p] // SIDE, roots[p] % SIDE
        place.append(lax.rem(x - rx + SIDE, SIDE) * SIDE + lax.rem(y - ry + SIDE, SIDE))
        load = pltpu.make_async_copy(slot_ref.at[0], panel.at[p], load_sem.at[1])

        @pl.when(place[p] == 0)
        def _():
            load.start()
            load.wait()

    pl.semaphore_wait(barrier, GRID - 1 + DEPTH - 1 + 1)
    level = [[sum(bit(m, place[p]) for m in DEEPER[t]) for t in range(TREES)] for p in range(PANELS)]

    def piece(p, c, t, d):
        ref = panel.at[p, pl.ds(pl.multiple_of((c * TREES + t) * CHUNK, CHUNK), CHUNK)]
        return pltpu.make_async_remote_copy(
            src_ref=ref, dst_ref=ref, send_sem=tree_send.at[p, t, d], recv_sem=tree_recv.at[p, c, t],
            device_id={"col": near[d]}, device_id_type=MESH,
        )

    def spread(s):
        for p in range(PANELS):
            for t in range(TREES):
                c = s - p * count - SKEW * level[p][t]

                @pl.when(jnp.logical_and(c >= 0, c < count))
                def _():
                    @pl.when(place[p] != 0)
                    def _():
                        piece(p, c, t, 0).wait_recv()

                    for d in range(4):
                        @pl.when(bit(CHILD[t][d], place[p]) == 1)
                        def _():
                            piece(p, c, t, d).start()

    part = rows // PREP

    def prepare(i):
        at = pl.ds(pl.multiple_of(i * part, part), part)
        high, low = split(state[at, :].T)
        xh[0:width, at] = high
        xl[0:width, at] = low

    pick = lax.broadcasted_iota(jnp.int32, (16, NB), 0)
    pick = jnp.where(pick < 8, 0, HALF - 8) + pick + 8 * col
    pick = jnp.where(pick == lax.broadcasted_iota(jnp.int32, (16, NB), 1), 1.0, 0.0).astype(jnp.bfloat16)

    def gather(p, c):
        at = pl.ds(pl.multiple_of(c * block, block), block)
        high, low = split(panel[p, at, :])
        vh[p, at, :] = high
        vl[p, at, :] = low
        tall = width if p == 0 else width + 32
        acc[p, 0:tall, :] += dot3((xh[0:tall, at], xl[0:tall, at]), (high, low))
        if p < PANELS - 1:
            strip = slice(width + 16 * p, width + 16 * p + 16)
            xh[strip, at] = dot(pick, high, True).astype(jnp.bfloat16)
            xl[strip, at] = dot(pick, low, True).astype(jnp.bfloat16)

    def remote(src, dst, send, recv, device):
        return pltpu.make_async_remote_copy(
            src_ref=src, dst_ref=dst, send_sem=send, recv_sem=recv, device_id=device, device_id_type=MESH
        )

    def to_mate(p):
        copies = [remote(acc.at[p, pl.ds(pl.multiple_of((1 - core) * half, half), half)], fromcore.at[p, pl.ds(0, half)],
                         core_send.at[p, 0], core_recv.at[p, 0], mate)]
        if p:
            copies.append(remote(acc.at[p, pl.ds(width, 32)], fromcore.at[p, pl.ds(half, 32)],
                                 core_send.at[p, 1], core_recv.at[p, 1], mate))
        return copies

    half = width // 2
    slice_rows = half // DEPTH

    def z_out(p):
        copies = []
        for k in range(1, DEPTH):
            there = {"row": zplus(k) * 2 + core}
            copies.append(remote(chip.at[p, pl.ds(pl.multiple_of(zplus(k) * slice_rows, slice_rows), slice_rows)],
                                 fromz.at[p, k], z_send.at[p, k], z_recv.at[p, k], there))
            if p:
                copies.append(remote(chip.at[p, pl.ds(half, 16)], crossz.at[p - 1, k],
                                     cz_send.at[p, k], cz_recv.at[p, k], there))
        return copies

    def mine(p, k):
        at = core * half + zplus(DEPTH - k) * slice_rows
        return total.at[p, pl.ds(pl.multiple_of(at, slice_rows), slice_rows)]

    def all_out(p):
        return [remote(mine(p, 0), mine(p, 0), all_send.at[p, k], all_recv.at[p, k], {"row": zplus(k) * 2 + core})
                for k in range(1, DEPTH)]

    def relay_out(p, k):
        return remote(mine(p, k), mine(p, k), relay_send.at[p, k], relay_recv.at[p, k], mate)

    def plane_out(p):
        ref = cross.at[p - 1, core, col]
        return [remote(ref, ref, plane_send.at[p, k], plane_recv.at[p, k], {"col": lax.rem(col + k, GRID)})
                for k in range(1, GRID)]

    def pass_out(p):
        ref = cross.at[p - 1, core]
        return remote(ref, ref, pass_send.at[p], pass_recv.at[p], mate)

    def stage_a(p):
        for copy in to_mate(p):
            copy.start()

    def stage_b(p):
        for copy in to_mate(p):
            copy.wait_recv()
        chip[p, 0:half, :] = acc[p, pl.ds(pl.multiple_of(core * half, half), half), :] + fromcore[p, 0:half, :]
        if p:
            for q in range(2):
                at = pl.multiple_of(16 * q + 8 * core, 8)
                chip[p, half + 8 * q : half + 8 * q + 8, :] = (
                    acc[p, pl.ds(width + at, 8), :] + fromcore[p, pl.ds(half + at, 8), :]
                )
        for copy in z_out(p):
            copy.start()

    def stage_d(p):
        for copy in z_out(p):
            copy.wait_recv()
        own = chip[p, pl.ds(pl.multiple_of(z * slice_rows, slice_rows), slice_rows), :]
        for k in range(1, DEPTH):
            own = own + fromz[p, k]
        at = pl.multiple_of(core * half + z * slice_rows, slice_rows)
        total[p, pl.ds(at, slice_rows), :] = own
        for copy in all_out(p):
            copy.start()
        relay_out(p, 0).start()
        if p:
            for q in range(2):
                own = chip[p, half + 8 * q : half + 8 * q + 8, :]
                for k in range(1, DEPTH):
                    own = own + crossz[p - 1, k, 8 * q : 8 * q + 8, :]
                cross[p - 1, core, col, q] = own
            for copy in plane_out(p):
                copy.start()

    def stage_f(p):
        for k, copy in enumerate(all_out(p), 1):
            copy.wait_recv()
            relay_out(p, k).start()
        if p:
            for copy in plane_out(p):
                copy.wait_recv()
            pass_out(p).start()

    def stage_g(p):
        for k in range(DEPTH):
            relay_out(p, k).wait_recv()
        if p:
            pass_out(p).wait_recv()
        inner = total[p]
        for q in range(p):
            mixed = cross[p - 1, :, :, q].reshape(NB, NB)
            inner = inner - dot3((yth[q], ytl[q]), split(mixed))
        scaled = dot3(split(inner), split(t_ref[p]), True)
        if p < PANELS - 1:
            yth[p], ytl[p] = split(scaled)
        yh[...], yl[...] = split(scaled.T)

        def update(i, carry):
            at = pl.ds(pl.multiple_of(i * 256, 256), 256)
            state[at, :] = state[at, :] - dot3((vh[p, at, :], vl[p, at, :]), (yh[...], yl[...]))
            if p == PANELS - 1:
                pltpu.make_async_copy(state.at[at], out_ref.at[at], out_sem.at[i]).start()
            return carry

        lax.fori_loop(0, rows // 256, update, 0)

    zeros = jnp.zeros((32, rows), jnp.bfloat16)
    xh[width : width + 32, :] = zeros
    xl[width : width + 32, :] = zeros
    acc[...] = jnp.zeros_like(acc)
    load_x.wait()

    fill = SKEW * HOPS
    steps = PANELS * count + fill
    plan = []
    for p in range(PANELS):
        end = (p + 1) * count + fill
        for stage, gap in ((stage_a, 0), (stage_b, GAPS[0]), (stage_d, GAPS[1]), (stage_f, GAPS[2]), (stage_g, GAPS[3])):
            plan.append((end + gap, p, stage))
    plan.sort(key=lambda entry: entry[:2])
    late = [entry for entry in plan if entry[0] >= steps]
    plan = [entry for entry in plan if entry[0] < steps]
    cuts = sorted({0, min(PREP, fill), fill, steps} | {fill + p * count for p in range(1, PANELS)} | {entry[0] for entry in plan})
    for low, high in zip(cuts, cuts[1:]):
        for step, p, stage in plan:
            if step == low:
                stage(p)

        def turn_step(s, carry):
            spread(s)
            if low < PREP and low < fill:
                prepare(s)
            if low >= fill:
                p = (low - fill) // count
                gather(p, s - fill - p * count)
            return carry

        lax.fori_loop(low, high, turn_step, 0)

    order = [(stage_a, 2), (stage_b, 1), (stage_d, 0), (stage_d, 1), (stage_b, 2), (stage_f, 0), (stage_g, 0), (stage_f, 1),
             (stage_g, 1), (stage_d, 2), (stage_f, 2), (stage_g, 2)]
    pending = {(stage, p) for _, p, stage in late}
    for stage, p in order:
        if (stage, p) in pending:
            stage(p)

    for p in range(PANELS):
        for t in range(TREES):
            for d in range(4):
                @pl.when(bit(CHILD[t][d], place[p]) == 1)
                def _():
                    whole = panel.at[p, pl.ds(0, rows // TREES)]
                    remote(whole, whole, tree_send.at[p, t, d], tree_recv.at[p, 0, t], {"col": near[d]}).wait_send()
        for copy in to_mate(p) + z_out(p) + all_out(p) + [relay_out(p, k) for k in range(DEPTH)]:
            copy.wait_send()
        if p:
            for copy in plane_out(p) + [pass_out(p)]:
                copy.wait_send()
    for i in range(rows // 256):
        at = pl.ds(i * 256, 256)
        pltpu.make_async_copy(state.at[at], out_ref.at[at], out_sem.at[i]).wait()


def transform(roots, key, slot, eigvec, tfac):
    rows, width = eigvec.shape
    count = rows // (TREES * CHUNK)
    f32, bf16 = jnp.float32, jnp.bfloat16
    dma = pltpu.SemaphoreType.DMA
    return pl.pallas_call(
        functools.partial(kernel, roots),
        out_shape=jax.ShapeDtypeStruct((rows, width), f32),
        in_specs=[pl.BlockSpec(memory_space=pl.ANY), pl.BlockSpec(memory_space=pl.ANY), pl.BlockSpec(memory_space=pltpu.VMEM)],
        out_specs=pl.BlockSpec(memory_space=pl.ANY),
        scratch_shapes=[
            pltpu.VMEM((PANELS, rows, NB), f32),
            pltpu.VMEM((rows, width), f32),
            pltpu.VMEM((width + 32, rows), bf16),
            pltpu.VMEM((width + 32, rows), bf16),
            pltpu.VMEM((PANELS, rows, NB), bf16),
            pltpu.VMEM((PANELS, rows, NB), bf16),
            pltpu.VMEM((PANELS, width + 32, NB), f32),
            pltpu.VMEM((PANELS, width // 2 + 32, NB), f32),
            pltpu.VMEM((PANELS, width // 2 + 16, NB), f32),
            pltpu.VMEM((PANELS, DEPTH, width // 2 // DEPTH, NB), f32),
            pltpu.VMEM((PANELS - 1, DEPTH, 16, NB), f32),
            pltpu.VMEM((PANELS, width, NB), f32),
            pltpu.VMEM((PANELS - 1, 2, GRID, 2, 8, NB), f32),
            pltpu.VMEM((PANELS - 1, width, NB), bf16),
            pltpu.VMEM((PANELS - 1, width, NB), bf16),
            pltpu.VMEM((NB, width), bf16),
            pltpu.VMEM((NB, width), bf16),
            dma((PANELS, TREES, 4)),
            dma((PANELS, count, TREES)),
            dma((2,)),
            dma((PANELS, 2)), dma((PANELS, 2)),
            dma((PANELS, DEPTH)), dma((PANELS, DEPTH)),
            dma((PANELS, DEPTH)), dma((PANELS, DEPTH)),
            dma((PANELS, DEPTH)), dma((PANELS, DEPTH)),
            dma((PANELS, DEPTH)), dma((PANELS, DEPTH)),
            dma((PANELS, GRID)), dma((PANELS, GRID)),
            dma((PANELS,)), dma((PANELS,)),
            dma((rows // 256,)),
        ],
        compiler_params=pltpu.CompilerParams(
            collective_id=key, has_side_effects=True, vmem_limit_bytes=60 << 20
        ),
        name="transform_%d" % key,
    )(slot, eigvec, tfac)


def shards(eigvec, slots, roots, tfac):
    return lax.cond(
        roots[0] == GRID - 2,
        functools.partial(transform, (GRID - 2, GRID - 1, 0), 0),
        functools.partial(transform, (GRID - 1, 0, 1), 1),
        slots, eigvec, tfac,
    )


def solution(mesh):
    in_specs = (P("row", "col"), P("col", "row", None), P(), P())
    out_specs = P("row", "col")
    return jax.shard_map(shards, mesh=mesh, in_specs=in_specs, out_specs=out_specs, check_vma=False)
```

```python
import functools

import jax
import jax.numpy as jnp
from jax import lax
from jax.experimental import pallas as pl
from jax.experimental.pallas import tpu as pltpu
from jax.sharding import PartitionSpec as P

PANELS = 3
NB = 256
SIDE = 4
TREES = 4
HOPS = 5
CHUNK = 128
LAGS = (0, 3, 6, 9, 12, 15)
UNITS = 2 * PANELS
GRID = SIDE * SIDE
DEPTH = 8
HALF = NB // 2
TILE = 512
TAIL = (
    ("a", 5), ("b", 4), ("d", 2), ("d", 3), ("f", 2), ("f", 3), ("b", 5), ("g", 0), ("g", 1), ("d", 4),
    ("g", 2), ("g", 3), ("d", 5), ("f", 4), ("g", 4), ("f", 5), ("g", 5),
)
PREP = 8
GAPS = (2, 6, 11, 12)
MESH = pl.DeviceIdType.MESH

FEED = {
    (0, 1): 0, (0, 2): 0, (0, 3): 0, (1, 0): 2, (1, 1): 2, (1, 2): 2, (1, 3): 2, (2, 0): 2,
    (2, 1): 1, (2, 2): 1, (2, 3): 2, (3, 0): 2, (3, 1): 1, (3, 2): 3, (3, 3): 3,
}
STEP = ((1, 0), (0, 1), (-1, 0), (0, -1))


def turn(node, times):
    for _ in range(times):
        node = (-node[1] % SIDE, node[0])
    return node


def build_tables():
    depth = {(0, 0): 0}

    def find(node):
        if node not in depth:
            dx, dy = STEP[FEED[node]]
            depth[node] = 1 + find(((node[0] - dx) % SIDE, (node[1] - dy) % SIDE))
        return depth[node]

    child = [[0] * 4 for _ in range(TREES)]
    deeper = [[0] * HOPS for _ in range(TREES)]
    for node in FEED:
        find(node)
        dx, dy = STEP[FEED[node]]
        parent = ((node[0] - dx) % SIDE, (node[1] - dy) % SIDE)
        for t in range(TREES):
            px, py = turn(parent, t)
            child[t][(FEED[node] + t) % 4] |= 1 << (px * SIDE + py)
            nx, ny = turn(node, t)
            for level in range(depth[node]):
                deeper[t][level] |= 1 << (nx * SIDE + ny)
    return child, deeper


CHILD, DEEPER = build_tables()


def bit(mask, place):
    return lax.rem(lax.shift_right_logical(jnp.int32(mask), place), 2)


def split(value):
    high = value.astype(jnp.bfloat16)
    return high, (value - high.astype(jnp.float32)).astype(jnp.bfloat16)


def dot(left, right, turned=False):
    dims = ((1,), (1,)) if turned else ((1,), (0,))
    return lax.dot_general(left, right, (dims, ((), ())), preferred_element_type=jnp.float32)


def dot3(left, right, turned=False):
    return dot(left[0], right[0], turned) + (dot(left[0], right[1], turned) + dot(left[1], right[0], turned))


def kernel(
    roots, slot_ref, x_ref, t_ref, state_out, panel_out, y_out,
    panel, state, xh, xl, vh, vl, acc, fromcore, chip, fromz, crossz, total, cross, yth, ytl, yh, yl,
    tree_send, tree_recv, load_sem, core_send, core_recv, z_send, z_recv, cz_send, cz_recv,
    all_send, all_recv, relay_send, relay_recv, plane_send, plane_recv, pass_send, pass_recv, out_sem,
):
    row, col = lax.axis_index("row"), lax.axis_index("col")
    x, y = col // SIDE, lax.rem(col, SIDE)
    z, core = row // 2, lax.rem(row, 2)
    near = [
        lax.rem(x + 1, SIDE) * SIDE + y,
        x * SIDE + lax.rem(y + 1, SIDE),
        lax.rem(x + 3, SIDE) * SIDE + y,
        x * SIDE + lax.rem(y + 3, SIDE),
    ]
    mate = {"row": z * 2 + 1 - core}
    rows, width = state.shape
    block = TREES * CHUNK
    count = rows // block
    half = width // 2
    slice_rows = half // DEPTH
    fill = LAGS[HOPS]

    def zplus(k):
        return lax.rem(z + k, DEPTH)

    load_x = pltpu.make_async_copy(x_ref, state, load_sem.at[2])
    load_x.start()

    barrier = pltpu.get_barrier_semaphore()
    for k in range(1, GRID):
        pl.semaphore_signal(barrier, inc=1, device_id={"col": lax.rem(col + k, GRID)}, device_id_type=MESH)
    for k in range(1, DEPTH):
        pl.semaphore_signal(barrier, inc=1, device_id={"row": zplus(k) * 2 + core}, device_id_type=MESH)
    pl.semaphore_signal(barrier, inc=1, device_id=mate, device_id_type=MESH)

    place = []
    for p in range(PANELS):
        rx, ry = roots[p] // SIDE, roots[p] % SIDE
        place.append(lax.rem(x - rx + SIDE, SIDE) * SIDE + lax.rem(y - ry + SIDE, SIDE))

        @pl.when(place[p] == 0)
        def _():
            loads = [pltpu.make_async_copy(slot_ref.at[0, :, pl.ds(h * HALF, HALF)], panel.at[p, pl.ds(h * rows, rows)], load_sem.at[h])
                     for h in range(2)]
            for load in loads:
                load.start()
            for load in loads:
                load.wait()

    zeros = jnp.zeros((32, rows), jnp.bfloat16)
    xh[width : width + 32, :] = zeros
    xl[width : width + 32, :] = zeros
    acc[...] = jnp.zeros_like(acc)
    level = [[sum(bit(m, place[p]) for m in DEEPER[t]) for t in range(TREES)] for p in range(PANELS)]
    lag = [[sum(bit(m, place[p]) * (LAGS[i + 1] - LAGS[i]) for i, m in enumerate(DEEPER[t])) + 2 * p * count
            for t in range(TREES)] for p in range(PANELS)]
    feeds = [[[bit(CHILD[t][d], place[p]) == 1 for d in range(4)] for t in range(TREES)] for p in range(PANELS)]
    fed = [place[p] != 0 for p in range(PANELS)]
    load_x.wait()
    pl.semaphore_wait(barrier, GRID - 1 + DEPTH - 1 + 1)

    def piece(p, k, t, d):
        ref = panel.at[p, pl.ds(pl.multiple_of(k * block + t * CHUNK, CHUNK), CHUNK)]
        return pltpu.make_async_remote_copy(
            src_ref=ref, dst_ref=ref, send_sem=tree_send.at[p, t, d], recv_sem=tree_recv.at[p, k, t],
            device_id={"col": near[d]}, device_id_type=MESH,
        )

    def spread(s, low, high):
        for p in range(PANELS):
            if high <= 2 * p * count or low >= 2 * (p + 1) * count + fill:
                continue
            for t in range(TREES):
                k = s - lag[p][t]

                @pl.when(jnp.logical_and(k >= 0, k < 2 * count))
                def _():
                    @pl.when(fed[p])
                    def _():
                        piece(p, k, t, 0).wait_recv()

                    for d in range(4):
                        @pl.when(feeds[p][t][d])
                        def _():
                            piece(p, k, t, d).start()

    part = rows // PREP

    def prepare(i):
        at = pl.ds(pl.multiple_of(i * part, part), part)
        high, low = split(state[at, :].T)
        xh[0:width, at] = high
        xl[0:width, at] = low

    def chosen(h):
        line = lax.broadcasted_iota(jnp.int32, (16, HALF), 0)
        line = jnp.where(line // 8 == h, lax.rem(line, 8) + 8 * col, -1)
        line = jnp.where(line == lax.broadcasted_iota(jnp.int32, (16, HALF), 1), 1.0, 0.0)
        return line.astype(jnp.bfloat16)

    def gather(u, c):
        p, h = u // 2, u % 2
        at = pl.ds(pl.multiple_of(c * block, block), block)
        high, low = split(panel[p, pl.ds(pl.multiple_of(h * rows + c * block, block), block), :])
        vh[u, at, :] = high
        vl[u, at, :] = low
        tall = width if p == 0 else width + 32
        acc[u, 0:tall, :] += dot3((xh[0:tall, at], xl[0:tall, at]), (high, low))
        if p < PANELS - 1:
            strip = slice(width + 16 * p, width + 16 * p + 16)
            pick = chosen(h)
            for store, piece_of in ((xh, high), (xl, low)):
                picked = dot(pick, piece_of, True)
                if h:
                    picked = picked + store[strip, at].astype(jnp.float32)
                store[strip, at] = picked.astype(jnp.bfloat16)

    def remote(src, dst, send, recv, device):
        return pltpu.make_async_remote_copy(
            src_ref=src, dst_ref=dst, send_sem=send, recv_sem=recv, device_id=device, device_id_type=MESH
        )

    def to_mate(u):
        copies = [remote(acc.at[u, pl.ds(pl.multiple_of((1 - core) * half, half), half)], fromcore.at[u, pl.ds(0, half)],
                         core_send.at[u, 0], core_recv.at[u, 0], mate)]
        if u > 1:
            copies.append(remote(acc.at[u, pl.ds(width, 32)], fromcore.at[u, pl.ds(half, 32)],
                                 core_send.at[u, 1], core_recv.at[u, 1], mate))
        return copies

    def z_out(u):
        copies = []
        for k in range(1, DEPTH):
            there = {"row": zplus(k) * 2 + core}
            copies.append(remote(chip.at[u, pl.ds(pl.multiple_of(zplus(k) * slice_rows, slice_rows), slice_rows)],
                                 fromz.at[u, k], z_send.at[u, k], z_recv.at[u, k], there))
            if u > 1:
                tall = 8 * (u // 2)
                copies.append(remote(chip.at[u, pl.ds(half, tall)], crossz.at[u - 2, k, pl.ds(0, tall)],
                                     cz_send.at[u, k], cz_recv.at[u, k], there))
        return copies

    def mine(u, k):
        at = core * half + zplus(DEPTH - k) * slice_rows
        return total.at[u, pl.ds(pl.multiple_of(at, slice_rows), slice_rows)]

    def all_out(u):
        return [remote(mine(u, 0), mine(u, 0), all_send.at[u, k], all_recv.at[u, k], {"row": zplus(k) * 2 + core})
                for k in range(1, DEPTH)]

    def relay_out(u, k):
        return remote(mine(u, k), mine(u, k), relay_send.at[u, k], relay_recv.at[u, k], mate)

    def plane_out(u):
        ref = cross.at[u - 2, core, col]
        return [remote(ref, ref, plane_send.at[u - 2, k], plane_recv.at[u - 2, k], {"col": lax.rem(col + k, GRID)})
                for k in range(1, GRID)]

    def pass_out(u):
        ref = cross.at[u - 2, core]
        return remote(ref, ref, pass_send.at[u - 2], pass_recv.at[u - 2], mate)

    def stage_a(u):
        for copy in to_mate(u):
            copy.start()

    def stage_b(u):
        for copy in to_mate(u):
            copy.wait_recv()
        chip[u, 0:half, :] = acc[u, pl.ds(pl.multiple_of(core * half, half), half), :] + fromcore[u, 0:half, :]
        for q in range(u // 2):
            at = pl.multiple_of(16 * q + 8 * core, 8)
            chip[u, half + 8 * q : half + 8 * q + 8, :] = (
                acc[u, pl.ds(width + at, 8), :] + fromcore[u, pl.ds(half + at, 8), :]
            )
        for copy in z_out(u):
            copy.start()

    def stage_d(u):
        for copy in z_out(u):
            copy.wait_recv()
        own = chip[u, pl.ds(pl.multiple_of(z * slice_rows, slice_rows), slice_rows), :]
        for k in range(1, DEPTH):
            own = own + fromz[u, k]
        at = pl.multiple_of(core * half + z * slice_rows, slice_rows)
        total[u, pl.ds(at, slice_rows), :] = own
        for copy in all_out(u):
            copy.start()
        relay_out(u, 0).start()
        if u > 1:
            for q in range(2):
                if q < u // 2:
                    own = chip[u, half + 8 * q : half + 8 * q + 8, :]
                    for k in range(1, DEPTH):
                        own = own + crossz[u - 2, k, 8 * q : 8 * q + 8, :]
                else:
                    own = jnp.zeros((8, HALF), jnp.float32)
                cross[u - 2, core, col, q] = own
            for copy in plane_out(u):
                copy.start()

    def stage_f(u):
        for k, copy in enumerate(all_out(u), 1):
            copy.wait_recv()
            relay_out(u, k).start()
        if u > 1:
            for copy in plane_out(u):
                copy.wait_recv()
            pass_out(u).start()

    def stage_g(u):
        for k in range(DEPTH):
            relay_out(u, k).wait_recv()
        if u > 1:
            pass_out(u).wait_recv()
        if u % 2 == 0:
            return
        p = u // 2
        inner = jnp.concatenate([total[u - 1], total[u]], axis=1)
        for q in range(p):
            mixed = jnp.concatenate([cross[u - 3, :, :, q].reshape(NB, HALF), cross[u - 2, :, :, q].reshape(NB, HALF)], axis=1)
            inner = inner - dot3((yth[q], ytl[q]), split(mixed))
        scaled = dot3(split(inner), split(t_ref[p]), True)
        if p == PANELS - 1:
            y_out[...] = scaled.T
            return
        yth[p], ytl[p] = split(scaled)
        yh[...], yl[...] = split(scaled.T)

        def update(i, carry):
            at = pl.ds(pl.multiple_of(i * 256, 256), 256)
            high = jnp.concatenate([vh[u - 1, at, :], vh[u, at, :]], axis=1)
            low = jnp.concatenate([vl[u - 1, at, :], vl[u, at, :]], axis=1)
            state[at, :] = state[at, :] - dot3((high, low), (yh[...], yl[...]))
            return carry

        lax.fori_loop(0, rows // 256, update, 0)
        if p == PANELS - 2:
            pltpu.make_async_copy(state, state_out, out_sem.at[0]).start()

    steps = UNITS * count + fill
    plan = []
    for u in range(UNITS):
        end = (u + 1) * count + fill
        for stage, gap in ((stage_a, 0), (stage_b, GAPS[0]), (stage_d, GAPS[1]), (stage_f, GAPS[2]), (stage_g, GAPS[3])):
            plan.append((end + gap, u, stage))
    plan.sort(key=lambda entry: entry[:2])
    late = [entry for entry in plan if entry[0] >= steps]
    plan = [entry for entry in plan if entry[0] < steps]
    cuts = sorted({0, PREP, fill, steps} | {fill + u * count for u in range(1, UNITS)})
    for low, high in zip(cuts, cuts[1:]):
        def turn_step(s, carry):
            for step, u, stage in plan:
                if low <= step < high:
                    pl.when(s == step)(functools.partial(stage, u))
            spread(s, low, high)
            if low < PREP:
                prepare(s)
            if low >= fill:
                u = (low - fill) // count
                gather(u, s - fill - u * count)
            return carry

        lax.fori_loop(low, high, turn_step, 0)

    last = pltpu.make_async_copy(panel.at[PANELS - 1], panel_out, out_sem.at[1])
    last.start()
    pending = {(stage, u) for _, u, stage in late}
    for name, u in TAIL:
        stage = {"a": stage_a, "b": stage_b, "d": stage_d, "f": stage_f, "g": stage_g}[name]
        if (stage, u) in pending:
            stage(u)

    for p in range(PANELS):
        for t in range(TREES):
            for d in range(4):
                @pl.when(feeds[p][t][d])
                def _():
                    whole = panel.at[p, pl.ds(0, 2 * rows // TREES)]
                    remote(whole, whole, tree_send.at[p, t, d], tree_recv.at[p, 0, t], {"col": near[d]}).wait_send()
    for u in range(UNITS):
        for copy in to_mate(u) + z_out(u) + all_out(u) + [relay_out(u, k) for k in range(DEPTH)]:
            copy.wait_send()
        if u > 1:
            for copy in plane_out(u) + [pass_out(u)]:
                copy.wait_send()
    pltpu.make_async_copy(state, state_out, out_sem.at[0]).wait()
    last.wait()


def transform(roots, key, slot, eigvec, tfac):
    rows, width = eigvec.shape
    count = rows // (TREES * CHUNK)
    f32, bf16 = jnp.float32, jnp.bfloat16
    dma = pltpu.SemaphoreType.DMA
    anywhere = pl.BlockSpec(memory_space=pl.ANY)
    return pl.pallas_call(
        functools.partial(kernel, roots),
        out_shape=(
            jax.ShapeDtypeStruct((rows, width), f32),
            jax.ShapeDtypeStruct((2 * rows, HALF), f32),
            jax.ShapeDtypeStruct((NB, width), f32),
        ),
        in_specs=[anywhere, anywhere, pl.BlockSpec(memory_space=pltpu.VMEM)],
        out_specs=(anywhere, anywhere, pl.BlockSpec(memory_space=pltpu.VMEM)),
        scratch_shapes=[
            pltpu.VMEM((PANELS, 2 * rows, HALF), f32),
            pltpu.VMEM((rows, width), f32),
            pltpu.VMEM((width + 32, rows), bf16),
            pltpu.VMEM((width + 32, rows), bf16),
            pltpu.VMEM((UNITS, rows, HALF), bf16),
            pltpu.VMEM((UNITS, rows, HALF), bf16),
            pltpu.VMEM((UNITS, width + 32, HALF), f32),
            pltpu.VMEM((UNITS, width // 2 + 32, HALF), f32),
            pltpu.VMEM((UNITS, width // 2 + 16, HALF), f32),
            pltpu.VMEM((UNITS, DEPTH, width // 2 // DEPTH, HALF), f32),
            pltpu.VMEM((UNITS - 2, DEPTH, 16, HALF), f32),
            pltpu.VMEM((UNITS, width, HALF), f32),
            pltpu.VMEM((UNITS - 2, 2, GRID, 2, 8, HALF), f32),
            pltpu.VMEM((PANELS - 1, width, NB), bf16),
            pltpu.VMEM((PANELS - 1, width, NB), bf16),
            pltpu.VMEM((NB, width), bf16),
            pltpu.VMEM((NB, width), bf16),
            dma((PANELS, TREES, 4)),
            dma((PANELS, 2 * count, TREES)),
            dma((3,)),
            dma((UNITS, 2)), dma((UNITS, 2)),
            dma((UNITS, DEPTH)), dma((UNITS, DEPTH)),
            dma((UNITS, DEPTH)), dma((UNITS, DEPTH)),
            dma((UNITS, DEPTH)), dma((UNITS, DEPTH)),
            dma((UNITS, DEPTH)), dma((UNITS, DEPTH)),
            dma((UNITS - 2, GRID)), dma((UNITS - 2, GRID)),
            dma((UNITS - 2,)), dma((UNITS - 2,)),
            dma((2,)),
        ],
        compiler_params=pltpu.CompilerParams(
            collective_id=key, has_side_effects=True, vmem_limit_bytes=58 << 20
        ),
        name="transform_%d" % key,
    )(slot, eigvec, tfac)


def finish_kernel(state_ref, left_ref, right_ref, y_ref, out_ref, yh, yl):
    @pl.when(pl.program_id(0) == 0)
    def _():
        yh[...], yl[...] = split(y_ref[...])

    piece = split(jnp.concatenate([left_ref[...], right_ref[...]], axis=1))
    out_ref[...] = state_ref[...] - dot3(piece, (yh[...], yl[...]))


def finish(state, panel, scaled):
    rows, width = state.shape
    return pl.pallas_call(
        finish_kernel,
        out_shape=jax.ShapeDtypeStruct((rows, width), jnp.float32),
        grid=(rows // TILE,),
        in_specs=[
            pl.BlockSpec((TILE, width), lambda i: (i, 0)),
            pl.BlockSpec((TILE, HALF), lambda i: (i, 0)),
            pl.BlockSpec((TILE, HALF), lambda i: (i + rows // TILE, 0)),
            pl.BlockSpec((NB, width), lambda i: (0, 0)),
        ],
        out_specs=pl.BlockSpec((TILE, width), lambda i: (i, 0)),
        scratch_shapes=[pltpu.VMEM((NB, width), jnp.bfloat16), pltpu.VMEM((NB, width), jnp.bfloat16)],
        name="finish",
    )(state, panel, panel, scaled)


def shards(eigvec, slots, roots, tfac):
    state, panel, scaled = lax.cond(
        roots[0] == GRID - 2,
        functools.partial(transform, (GRID - 2, GRID - 1, 0), 0),
        functools.partial(transform, (GRID - 1, 0, 1), 1),
        slots, eigvec, tfac,
    )
    return finish(state, panel, scaled)


def solution(mesh):
    in_specs = (P("row", "col"), P("col", "row", None), P(), P())
    out_specs = P("row", "col")
    return jax.shard_map(shards, mesh=mesh, in_specs=in_specs, out_specs=out_specs, check_vma=False)
```

```python
import functools

import jax
import jax.numpy as jnp
from jax import lax
from jax.experimental import pallas as pl
from jax.experimental.pallas import tpu as pltpu
from jax.sharding import PartitionSpec as P

PANELS = 3
NB = 256
SIDE = 4
TREES = 4
HOPS = 5
CHUNK = 128
LAGS = (0, 3, 6, 9, 12, 15)
UNITS = 2 * PANELS
GRID = SIDE * SIDE
DEPTH = 8
HALF = NB // 2
TILE = 512
TAIL = (
    ("a", 5), ("b", 4), ("d", 2), ("d", 3), ("b", 5), ("f", 2), ("f", 3), ("g", 0), ("g", 1), ("d", 4),
    ("g", 2), ("g", 3), ("d", 5), ("f", 4), ("g", 4), ("f", 5), ("g", 5),
)
PREP = 8
GAPS = (2, 6, 11, 12)
MESH = pl.DeviceIdType.MESH

FEED = {
    (0, 1): 0, (0, 2): 0, (0, 3): 0, (1, 0): 2, (1, 1): 2, (1, 2): 2, (1, 3): 2, (2, 0): 2,
    (2, 1): 1, (2, 2): 1, (2, 3): 2, (3, 0): 2, (3, 1): 1, (3, 2): 3, (3, 3): 3,
}
STEP = ((1, 0), (0, 1), (-1, 0), (0, -1))


def turn(node, times):
    for _ in range(times):
        node = (-node[1] % SIDE, node[0])
    return node


def build_tables():
    depth = {(0, 0): 0}

    def find(node):
        if node not in depth:
            dx, dy = STEP[FEED[node]]
            depth[node] = 1 + find(((node[0] - dx) % SIDE, (node[1] - dy) % SIDE))
        return depth[node]

    child = [[0] * 4 for _ in range(TREES)]
    deeper = [[0] * HOPS for _ in range(TREES)]
    for node in FEED:
        find(node)
        dx, dy = STEP[FEED[node]]
        parent = ((node[0] - dx) % SIDE, (node[1] - dy) % SIDE)
        for t in range(TREES):
            px, py = turn(parent, t)
            child[t][(FEED[node] + t) % 4] |= 1 << (px * SIDE + py)
            nx, ny = turn(node, t)
            for level in range(depth[node]):
                deeper[t][level] |= 1 << (nx * SIDE + ny)
    return child, deeper


CHILD, DEEPER = build_tables()


def bit(mask, place):
    return lax.rem(lax.shift_right_logical(jnp.int32(mask), place), 2)


def split(value):
    high = value.astype(jnp.bfloat16)
    return high, (value - high.astype(jnp.float32)).astype(jnp.bfloat16)


def dot(left, right, turned=False):
    dims = ((1,), (1,)) if turned else ((1,), (0,))
    return lax.dot_general(left, right, (dims, ((), ())), preferred_element_type=jnp.float32)


def dot3(left, right, turned=False):
    return dot(left[0], right[0], turned) + (dot(left[0], right[1], turned) + dot(left[1], right[0], turned))


def kernel(
    roots, slot_ref, x_ref, t_ref, state_out, panel_out, y_out,
    panel, state, xh, xl, vh, vl, acc, fromcore, chip, fromz, crossz, total, cross, yth, ytl, yh, yl,
    tree_send, tree_recv, load_sem, core_send, core_recv, z_send, z_recv, cz_send, cz_recv,
    all_send, all_recv, relay_send, relay_recv, plane_send, plane_recv, pass_send, pass_recv, out_sem,
):
    row, col = lax.axis_index("row"), lax.axis_index("col")
    x, y = col // SIDE, lax.rem(col, SIDE)
    z, core = row // 2, lax.rem(row, 2)
    near = [
        lax.rem(x + 1, SIDE) * SIDE + y,
        x * SIDE + lax.rem(y + 1, SIDE),
        lax.rem(x + 3, SIDE) * SIDE + y,
        x * SIDE + lax.rem(y + 3, SIDE),
    ]
    mate = {"row": z * 2 + 1 - core}
    rows, width = state.shape
    block = TREES * CHUNK
    count = rows // block
    half = width // 2
    slice_rows = half // DEPTH
    fill = LAGS[HOPS]

    def zplus(k):
        return lax.rem(z + k, DEPTH)

    load_x = pltpu.make_async_copy(x_ref, state, load_sem.at[2])
    load_x.start()

    barrier = pltpu.get_barrier_semaphore()
    for k in range(1, GRID):
        pl.semaphore_signal(barrier, inc=1, device_id={"col": lax.rem(col + k, GRID)}, device_id_type=MESH)
    for k in range(1, DEPTH):
        pl.semaphore_signal(barrier, inc=1, device_id={"row": zplus(k) * 2 + core}, device_id_type=MESH)
    pl.semaphore_signal(barrier, inc=1, device_id=mate, device_id_type=MESH)

    place = []
    for p in range(PANELS):
        rx, ry = roots[p] // SIDE, roots[p] % SIDE
        place.append(lax.rem(x - rx + SIDE, SIDE) * SIDE + lax.rem(y - ry + SIDE, SIDE))

        @pl.when(place[p] == 0)
        def _():
            loads = [pltpu.make_async_copy(slot_ref.at[0, :, pl.ds(h * HALF, HALF)], panel.at[p, pl.ds(h * rows, rows)], load_sem.at[h])
                     for h in range(2)]
            for load in loads:
                load.start()
            for load in loads:
                load.wait()

    zeros = jnp.zeros((32, rows), jnp.bfloat16)
    xh[width : width + 32, :] = zeros
    xl[width : width + 32, :] = zeros
    acc[...] = jnp.zeros_like(acc)
    level = [[sum(bit(m, place[p]) for m in DEEPER[t]) for t in range(TREES)] for p in range(PANELS)]
    lag = [[sum(bit(m, place[p]) * (LAGS[i + 1] - LAGS[i]) for i, m in enumerate(DEEPER[t])) + 2 * p * count
            for t in range(TREES)] for p in range(PANELS)]
    feeds = [[[bit(CHILD[t][d], place[p]) == 1 for d in range(4)] for t in range(TREES)] for p in range(PANELS)]
    fed = [place[p] != 0 for p in range(PANELS)]
    load_x.wait()
    pl.semaphore_wait(barrier, GRID - 1 + DEPTH - 1 + 1)

    def piece(p, k, t, d):
        ref = panel.at[p, pl.ds(pl.multiple_of(k * block + t * CHUNK, CHUNK), CHUNK)]
        return pltpu.make_async_remote_copy(
            src_ref=ref, dst_ref=ref, send_sem=tree_send.at[p, t, d], recv_sem=tree_recv.at[p, k, t],
            device_id={"col": near[d]}, device_id_type=MESH,
        )

    def spread(s, low, high):
        for p in range(PANELS):
            if high <= 2 * p * count or low >= 2 * (p + 1) * count + fill:
                continue
            for t in range(TREES):
                k = s - lag[p][t]

                @pl.when(jnp.logical_and(k >= 0, k < 2 * count))
                def _():
                    @pl.when(fed[p])
                    def _():
                        piece(p, k, t, 0).wait_recv()

                    for d in range(4):
                        @pl.when(feeds[p][t][d])
                        def _():
                            piece(p, k, t, d).start()

    part = rows // PREP

    def prepare(i):
        at = pl.ds(pl.multiple_of(i * part, part), part)
        high, low = split(state[at, :].T)
        xh[0:width, at] = high
        xl[0:width, at] = low

    def chosen(h):
        line = lax.broadcasted_iota(jnp.int32, (16, HALF), 0)
        line = jnp.where(line // 8 == h, lax.rem(line, 8) + 8 * col, -1)
        line = jnp.where(line == lax.broadcasted_iota(jnp.int32, (16, HALF), 1), 1.0, 0.0)
        return line.astype(jnp.bfloat16)

    def gather(u, c):
        p, h = u // 2, u % 2
        at = pl.ds(pl.multiple_of(c * block, block), block)
        high, low = split(panel[p, pl.ds(pl.multiple_of(h * rows + c * block, block), block), :])
        vh[u, at, :] = high
        vl[u, at, :] = low
        tall = width if p == 0 else width + 32
        acc[u, 0:tall, :] += dot3((xh[0:tall, at], xl[0:tall, at]), (high, low))
        if p < PANELS - 1:
            strip = slice(width + 16 * p, width + 16 * p + 16)
            pick = chosen(h)
            for store, piece_of in ((xh, high), (xl, low)):
                picked = dot(pick, piece_of, True)
                if h:
                    picked = picked + store[strip, at].astype(jnp.float32)
                store[strip, at] = picked.astype(jnp.bfloat16)

    def remote(src, dst, send, recv, device):
        return pltpu.make_async_remote_copy(
            src_ref=src, dst_ref=dst, send_sem=send, recv_sem=recv, device_id=device, device_id_type=MESH
        )

    def to_mate(u):
        copies = [remote(acc.at[u, pl.ds(pl.multiple_of((1 - core) * half, half), half)], fromcore.at[u, pl.ds(0, half)],
                         core_send.at[u, 0], core_recv.at[u, 0], mate)]
        if u > 1:
            copies.append(remote(acc.at[u, pl.ds(width, 32)], fromcore.at[u, pl.ds(half, 32)],
                                 core_send.at[u, 1], core_recv.at[u, 1], mate))
        return copies

    def z_out(u):
        copies = []
        for k in range(1, DEPTH):
            there = {"row": zplus(k) * 2 + core}
            copies.append(remote(chip.at[u, pl.ds(pl.multiple_of(zplus(k) * slice_rows, slice_rows), slice_rows)],
                                 fromz.at[u, k], z_send.at[u, k], z_recv.at[u, k], there))
            if u > 1:
                tall = 8 * (u // 2)
                copies.append(remote(chip.at[u, pl.ds(half, tall)], crossz.at[u - 2, k, pl.ds(0, tall)],
                                     cz_send.at[u, k], cz_recv.at[u, k], there))
        return copies

    def mine(u, k):
        at = core * half + zplus(DEPTH - k) * slice_rows
        return total.at[u, pl.ds(pl.multiple_of(at, slice_rows), slice_rows)]

    def all_out(u):
        return [remote(mine(u, 0), mine(u, 0), all_send.at[u, k], all_recv.at[u, k], {"row": zplus(k) * 2 + core})
                for k in range(1, DEPTH)]

    def relay_out(u, k):
        return remote(mine(u, k), mine(u, k), relay_send.at[u, k], relay_recv.at[u, k], mate)

    def plane_out(u):
        ref = cross.at[u - 2, core, col]
        return [remote(ref, ref, plane_send.at[u - 2, k], plane_recv.at[u - 2, k], {"col": lax.rem(col + k, GRID)})
                for k in range(1, GRID)]

    def pass_out(u):
        ref = cross.at[u - 2, core]
        return remote(ref, ref, pass_send.at[u - 2], pass_recv.at[u - 2], mate)

    def stage_a(u):
        for copy in to_mate(u):
            copy.start()

    def stage_b(u):
        for copy in to_mate(u):
            copy.wait_recv()
        chip[u, 0:half, :] = acc[u, pl.ds(pl.multiple_of(core * half, half), half), :] + fromcore[u, 0:half, :]
        for q in range(u // 2):
            at = pl.multiple_of(16 * q + 8 * core, 8)
            chip[u, half + 8 * q : half + 8 * q + 8, :] = (
                acc[u, pl.ds(width + at, 8), :] + fromcore[u, pl.ds(half + at, 8), :]
            )
        for copy in z_out(u):
            copy.start()

    def stage_d(u):
        for copy in z_out(u):
            copy.wait_recv()
        own = chip[u, pl.ds(pl.multiple_of(z * slice_rows, slice_rows), slice_rows), :]
        for k in range(1, DEPTH):
            own = own + fromz[u, k]
        at = pl.multiple_of(core * half + z * slice_rows, slice_rows)
        total[u, pl.ds(at, slice_rows), :] = own
        for copy in all_out(u):
            copy.start()
        relay_out(u, 0).start()
        if u > 1:
            for q in range(2):
                if q < u // 2:
                    own = chip[u, half + 8 * q : half + 8 * q + 8, :]
                    for k in range(1, DEPTH):
                        own = own + crossz[u - 2, k, 8 * q : 8 * q + 8, :]
                else:
                    own = jnp.zeros((8, HALF), jnp.float32)
                cross[u - 2, core, col, q] = own
            for copy in plane_out(u):
                copy.start()

    def stage_f(u):
        for k, copy in enumerate(all_out(u), 1):
            copy.wait_recv()
            relay_out(u, k).start()
        if u > 1:
            for copy in plane_out(u):
                copy.wait_recv()
            pass_out(u).start()

    def stage_g(u):
        for k in range(DEPTH):
            relay_out(u, k).wait_recv()
        if u > 1:
            pass_out(u).wait_recv()
        if u % 2 == 0:
            return
        p = u // 2
        inner = jnp.concatenate([total[u - 1], total[u]], axis=1)
        for q in range(p):
            mixed = jnp.concatenate([cross[u - 3, :, :, q].reshape(NB, HALF), cross[u - 2, :, :, q].reshape(NB, HALF)], axis=1)
            inner = inner - dot3((yth[q], ytl[q]), split(mixed))
        scaled = dot3(split(inner), split(t_ref[p]), True)
        if p == PANELS - 1:
            y_out[...] = scaled.T
            return
        yth[p], ytl[p] = split(scaled)
        yh[...], yl[...] = split(scaled.T)

        def update(i, carry):
            at = pl.ds(pl.multiple_of(i * 256, 256), 256)
            high = jnp.concatenate([vh[u - 1, at, :], vh[u, at, :]], axis=1)
            low = jnp.concatenate([vl[u - 1, at, :], vl[u, at, :]], axis=1)
            state[at, :] = state[at, :] - dot3((high, low), (yh[...], yl[...]))
            return carry

        lax.fori_loop(0, rows // 256, update, 0)
        if p == PANELS - 2:
            pltpu.make_async_copy(state, state_out, out_sem.at[0]).start()

    steps = UNITS * count + fill
    plan = []
    for u in range(UNITS):
        end = (u + 1) * count + fill
        for stage, gap in ((stage_a, 0), (stage_b, GAPS[0]), (stage_d, GAPS[1]), (stage_f, GAPS[2]), (stage_g, GAPS[3])):
            plan.append((end + gap, u, stage))
    plan.sort(key=lambda entry: entry[:2])
    late = [entry for entry in plan if entry[0] >= steps]
    plan = [entry for entry in plan if entry[0] < steps]
    cuts = sorted({0, PREP, fill, steps} | {fill + u * count for u in range(1, UNITS)})
    for low, high in zip(cuts, cuts[1:]):
        def turn_step(s, carry):
            for step, u, stage in plan:
                if low <= step < high:
                    pl.when(s == step)(functools.partial(stage, u))
            spread(s, low, high)
            if low < PREP:
                prepare(s)
            if low >= fill:
                u = (low - fill) // count
                gather(u, s - fill - u * count)
            return carry

        lax.fori_loop(low, high, turn_step, 0)

    last = pltpu.make_async_copy(panel.at[PANELS - 1], panel_out, out_sem.at[1])
    last.start()
    pending = {(stage, u) for _, u, stage in late}
    for name, u in TAIL:
        stage = {"a": stage_a, "b": stage_b, "d": stage_d, "f": stage_f, "g": stage_g}[name]
        if (stage, u) in pending:
            stage(u)

    for p in range(PANELS):
        for t in range(TREES):
            for d in range(4):
                @pl.when(feeds[p][t][d])
                def _():
                    whole = panel.at[p, pl.ds(0, 2 * rows // TREES)]
                    remote(whole, whole, tree_send.at[p, t, d], tree_recv.at[p, 0, t], {"col": near[d]}).wait_send()
    for u in range(UNITS):
        for copy in to_mate(u) + z_out(u) + all_out(u) + [relay_out(u, k) for k in range(DEPTH)]:
            copy.wait_send()
        if u > 1:
            for copy in plane_out(u) + [pass_out(u)]:
                copy.wait_send()
    pltpu.make_async_copy(state, state_out, out_sem.at[0]).wait()
    last.wait()


def transform(roots, key, slot, eigvec, tfac):
    rows, width = eigvec.shape
    count = rows // (TREES * CHUNK)
    f32, bf16 = jnp.float32, jnp.bfloat16
    dma = pltpu.SemaphoreType.DMA
    anywhere = pl.BlockSpec(memory_space=pl.ANY)
    return pl.pallas_call(
        functools.partial(kernel, roots),
        out_shape=(
            jax.ShapeDtypeStruct((rows, width), f32),
            jax.ShapeDtypeStruct((2 * rows, HALF), f32),
            jax.ShapeDtypeStruct((NB, width), f32),
        ),
        in_specs=[anywhere, anywhere, pl.BlockSpec(memory_space=pltpu.VMEM)],
        out_specs=(anywhere, anywhere, pl.BlockSpec(memory_space=pltpu.VMEM)),
        scratch_shapes=[
            pltpu.VMEM((PANELS, 2 * rows, HALF), f32),
            pltpu.VMEM((rows, width), f32),
            pltpu.VMEM((width + 32, rows), bf16),
            pltpu.VMEM((width + 32, rows), bf16),
            pltpu.VMEM((UNITS, rows, HALF), bf16),
            pltpu.VMEM((UNITS, rows, HALF), bf16),
            pltpu.VMEM((UNITS, width + 32, HALF), f32),
            pltpu.VMEM((UNITS, width // 2 + 32, HALF), f32),
            pltpu.VMEM((UNITS, width // 2 + 16, HALF), f32),
            pltpu.VMEM((UNITS, DEPTH, width // 2 // DEPTH, HALF), f32),
            pltpu.VMEM((UNITS - 2, DEPTH, 16, HALF), f32),
            pltpu.VMEM((UNITS, width, HALF), f32),
            pltpu.VMEM((UNITS - 2, 2, GRID, 2, 8, HALF), f32),
            pltpu.VMEM((PANELS - 1, width, NB), bf16),
            pltpu.VMEM((PANELS - 1, width, NB), bf16),
            pltpu.VMEM((NB, width), bf16),
            pltpu.VMEM((NB, width), bf16),
            dma((PANELS, TREES, 4)),
            dma((PANELS, 2 * count, TREES)),
            dma((3,)),
            dma((UNITS, 2)), dma((UNITS, 2)),
            dma((UNITS, DEPTH)), dma((UNITS, DEPTH)),
            dma((UNITS, DEPTH)), dma((UNITS, DEPTH)),
            dma((UNITS, DEPTH)), dma((UNITS, DEPTH)),
            dma((UNITS, DEPTH)), dma((UNITS, DEPTH)),
            dma((UNITS - 2, GRID)), dma((UNITS - 2, GRID)),
            dma((UNITS - 2,)), dma((UNITS - 2,)),
            dma((2,)),
        ],
        compiler_params=pltpu.CompilerParams(
            collective_id=key, has_side_effects=True, vmem_limit_bytes=58 << 20
        ),
        name="transform_%d" % key,
    )(slot, eigvec, tfac)


def finish_kernel(state_ref, left_ref, right_ref, y_ref, out_ref, yh, yl):
    @pl.when(pl.program_id(0) == 0)
    def _():
        yh[...], yl[...] = split(y_ref[...])

    piece = split(jnp.concatenate([left_ref[...], right_ref[...]], axis=1))
    out_ref[...] = state_ref[...] - dot3(piece, (yh[...], yl[...]))


def finish(state, panel, scaled):
    rows, width = state.shape
    return pl.pallas_call(
        finish_kernel,
        out_shape=jax.ShapeDtypeStruct((rows, width), jnp.float32),
        grid=(rows // TILE,),
        in_specs=[
            pl.BlockSpec((TILE, width), lambda i: (i, 0)),
            pl.BlockSpec((TILE, HALF), lambda i: (i, 0)),
            pl.BlockSpec((TILE, HALF), lambda i: (i + rows // TILE, 0)),
            pl.BlockSpec((NB, width), lambda i: (0, 0)),
        ],
        out_specs=pl.BlockSpec((TILE, width), lambda i: (i, 0)),
        scratch_shapes=[pltpu.VMEM((NB, width), jnp.bfloat16), pltpu.VMEM((NB, width), jnp.bfloat16)],
        name="finish",
    )(state, panel, panel, scaled)


def shards(eigvec, slots, roots, tfac):
    state, panel, scaled = lax.cond(
        roots[0] == GRID - 2,
        functools.partial(transform, (GRID - 2, GRID - 1, 0), 0),
        functools.partial(transform, (GRID - 1, 0, 1), 1),
        slots, eigvec, tfac,
    )
    return finish(state, panel, scaled)


def solution(mesh):
    in_specs = (P("row", "col"), P("col", "row", None), P(), P())
    out_specs = P("row", "col")
    return jax.shard_map(shards, mesh=mesh, in_specs=in_specs, out_specs=out_specs, check_vma=False)
```
